512 devices in a mesh: lon: 16 (over x_hi, y), lat: 32 (over x_lo, z, core).
Axes of the slice: x: 4 (x_hi: 2, x_lo: 2; x = x_hi * 2 + x_lo), y: 8, z: 8, core: 2. Of those that a mesh axis runs over, the one named last changes fastest.
Arguments:
- increment: float32 [64, 256, 4096], P(None, 'lat', 'lon'), may hold values from -6 to 6
- sea_levels: int32 [256, 4096], P('lat', 'lon'), may hold values from 0 to 64, as said below
- cell_sigma: float32 [256, 4096], P('lat', 'lon'), may hold values from 0.3 to 3
- level_sigma: float32 [64], replicated, may hold values from 0.5 to 2
- diffusivity: float32 [64, 256], replicated, may hold values from 0.04 to 0.45
- band_width: int32 [256], replicated, may hold values from 1 to 8, as said below
- vertical_root: float32 [64, 64], replicated
Outputs:
- covariance_product: float32 [64, 256, 4096], P(None, 'lat', 'lon')
The draws below stay inside these ranges and needn't reach their ends.
Inputs may be any that keep to these rules, and one draw needn't show every extreme that they name: `sea_levels`: some column has 64 sea levels and some are land. `band_width`: some row has half-width 8 and some row 1.
All inputs are finite; a program needn't handle non-finite values.
Results may differ from the reference program's by a relative error of at most 0.00008.
Values sent between devices are 32-bit elements; how exact they have to be, the bound alone decides.
A program may use at most 64 MiB of HBM per device.

```python
import math
import jax
import jax.numpy as jnp
from jax import lax

NZ = 64
WMAX = 8
STEPS = 4
NLAT = 256
NLON = 4096


def draw_sea_levels(key, part):
    first, second, third = jax.random.split(jax.random.fold_in(key, 11), 3)
    land = jax.random.randint(first, (NLAT, NLON), 0, 10) < 3
    depth = jax.random.randint(second, (NLAT, NLON), 1, NZ + 1)
    depth = jnp.where(land, 0, depth).astype(jnp.int32)
    spots = jax.random.randint(third, (4,), 0, NLAT * NLON)
    flat = depth.reshape(-1)
    flat = flat.at[spots[0]].set(NZ)
    flat = flat.at[spots[1]].set(0)
    return flat.reshape(NLAT, NLON).astype(jnp.int32)


def draw_band_width(key, part):
    first, second = jax.random.split(jax.random.fold_in(key, 23))
    widths = jax.random.randint(first, (NLAT,), 1, WMAX + 1)
    spot = jax.random.randint(second, (), 0, NLAT)
    widths = widths.at[spot].set(WMAX)
    widths = widths.at[(spot + 1) % NLAT].set(1)
    return widths.astype(jnp.int32)


def draw_vertical_root(key, part):
    first, second = jax.random.split(jax.random.fold_in(key, 37))
    spread = jax.random.normal(first, (NZ, NZ), jnp.float32) * (0.8 / NZ ** 0.5)
    diagonal = jax.random.uniform(second, (NZ,), jnp.float32, 1.0, 2.0)
    rows = lax.broadcasted_iota(jnp.int32, (NZ, NZ), 0)
    cols = lax.broadcasted_iota(jnp.int32, (NZ, NZ), 1)
    return jnp.where(rows == cols, diagonal[:, None] + 0.0 * spread, spread).astype(jnp.float32)


def shard_levels(own_key, shape, pieces, low, high):
    gain = 1.0
    for position, blocks in pieces:
        draws = jax.random.uniform(jax.random.fold_in(jax.random.fold_in(own_key, 6), position), (blocks,), jnp.float32, low / len(pieces), high / len(pieces))
        gain = gain * jnp.repeat(jnp.exp(draws), shape[position] // blocks).reshape((-1,) + (1,) * (len(shape) - 1 - position))
    return gain


def gaussian(key, shape, width, most, shards=(), dtype=jnp.bfloat16):
    array = width * jax.random.normal(key, shape, jnp.float32)
    if shards:
        array = array * shard_levels(key, shape, shards, -0.22, 0.18)
    return jnp.clip(array, -most, most).astype(dtype)


def setup_inputs(seed: int = 0) -> dict:
    seeds = jax.random.split(jax.random.key(seed), 8)
    return {
        "increment": gaussian(seeds[0], (NZ, NLAT, NLON), 1.0, 6.0, ((1, 32), (2, 16)), jnp.float32),
        "sea_levels": draw_sea_levels(jax.random.fold_in(seeds[7], 71), 0),
        "cell_sigma": jnp.clip(jnp.exp(math.log(3.0) - 2.3025851 * jax.random.uniform(seeds[2], (NLAT, NLON), jnp.float32) ** shard_levels(seeds[2], (NLAT, NLON), ((0, 32), (1, 16)), -0.2, 0.2)), 0.3, 3.0),
        "level_sigma": jnp.clip(jnp.exp(jax.random.uniform(seeds[3], (NZ,), jnp.float32, math.log(0.5), math.log(2.0))), 0.5, 2.0),
        "diffusivity": jnp.clip(jnp.exp(jax.random.uniform(seeds[4], (NZ, NLAT), jnp.float32, math.log(0.04), math.log(0.45))), 0.04, 0.45),
        "band_width": draw_band_width(jax.random.fold_in(seeds[7], 71), 0),
        "vertical_root": draw_vertical_root(jax.random.fold_in(seeds[7], 71), 0),
    }


def weights_for(band_rows, offset):
    widths = band_rows.astype(jnp.float32)
    return jnp.maximum(widths + 1.0 - abs(offset), 0.0) / ((widths + 1.0) * (widths + 1.0))


def zonal_ref(field, band_width):
    total = jnp.zeros_like(field)
    for offset in range(-WMAX, WMAX + 1):
        total = total + weights_for(band_width, offset)[None, :, None] * jnp.roll(field, -offset, axis=2)
    return total


def meridional(field, faces):
    for step in range(STEPS):
        flux = faces[:, :, None] * (field[:, 1:, :] - field[:, :-1, :])
        edge = jnp.zeros_like(field[:, :1, :])
        field = field + jnp.concatenate([flux, edge], axis=1) - jnp.concatenate([edge, flux], axis=1)
    return field


def reference(increment, sea_levels, cell_sigma, level_sigma, diffusivity, band_width, vertical_root):
    levels = lax.broadcasted_iota(jnp.int32, (NZ, 1, 1), 0)
    sea = (levels < sea_levels[None, :, :]).astype(jnp.float32)
    scale = level_sigma[:, None, None] * cell_sigma[None, :, :]
    field = increment * sea * scale
    field = jnp.einsum("lk,lji->kji", vertical_root, field, precision=lax.Precision.HIGHEST)
    faces = diffusivity[:, :-1]
    field = meridional(field, faces)
    field = zonal_ref(field, band_width)
    field = zonal_ref(field, band_width)
    field = meridional(field, faces)
    field = jnp.einsum("kl,lji->kji", vertical_root, field, precision=lax.Precision.HIGHEST)
    return field * scale * sea
```

```python
import functools

import jax
import jax.numpy as jnp
from jax import lax
from jax.experimental import pallas as pl
from jax.experimental.pallas import tpu as pltpu
from jax.sharding import PartitionSpec as P

STEPS = 4
HALO = 16
CHUNKS = 2
F32 = jnp.float32
BF16 = jnp.bfloat16
MESH = pl.DeviceIdType.MESH


def split(value):
    high = value.astype(BF16)
    return high, (value - high.astype(F32)).astype(BF16)


def dot(left, right):
    return jnp.dot(left, right, preferred_element_type=F32)


def band(distance, width):
    u = jnp.maximum(2.0 * width - 1.0 - jnp.abs(distance), 0.0)
    v = jnp.maximum(u - width, 0.0)
    return u * (u + 1.0) * (u + 2.0) - 4.0 * (v * (v + 1.0) * (v + 2.0))


def diffuse(rows, faces):
    for step in range(STEPS):
        flux = [faces[step + m] * (rows[m + 1] - rows[m]) for m in range(len(rows) - 1)]
        rows = [rows[m] + (flux[m] - flux[m - 1]) for m in range(1, len(rows) - 1)]
    return rows


def kernel(
    band_ref, inc_hbm, sea_ref, cell_ref, sigma_ref, diff_ref, root_ref, out_hbm,
    inc_ref, out_ref, first, second, mid, fin, edge, halo, faces_ref, w_high, w_low, zscale,
    load_sem, send_edge, recv_edge, send_lat, recv_lat,
):
    nz = root_ref.shape[0]
    lat_total = diff_ref.shape[1]
    part = nz // CHUNKS
    lat_count, lon_count = lax.axis_size("lat"), lax.axis_size("lon")
    lat, lon = lax.axis_index("lat"), lax.axis_index("lon")
    north, south = lax.rem(lat + 1, lat_count), lax.rem(lat + lat_count - 1, lat_count)
    east, west = lax.rem(lon + 1, lon_count), lax.rem(lon + lon_count - 1, lon_count)

    loads = [
        pltpu.make_async_copy(inc_hbm.at[:, pl.ds(128 * h, 128)], inc_ref.at[h], load_sem.at[h])
        for h in range(2)
    ]
    for load in loads:
        load.start()
    barrier = pltpu.get_barrier_semaphore()
    for a, o in (
        (north, lon), (south, lon), (lat, east), (lat, west),
        (north, east), (north, west), (south, east), (south, west),
    ):
        pl.semaphore_signal(barrier, inc=1, device_id={"lat": a, "lon": o}, device_id_type=MESH)

    lift = root_ref[...].T * sigma_ref[...]
    lift_high, lift_low = split(lift)
    lift3 = jnp.concatenate([lift_high, lift_high, lift_low], axis=1)
    lower_high, lower_low = split(lift.T)
    lower3 = jnp.concatenate([lower_high, lower_high, lower_low], axis=1)

    level = lax.broadcasted_iota(jnp.int32, (nz, 256), 0)
    lane128 = lax.broadcasted_iota(jnp.int32, (nz, 128), 1)

    for load in loads:
        load.wait()
    left_pack = jnp.zeros((nz, 128), F32)
    right_pack = jnp.zeros((nz, 128), F32)
    for j in range(8):
        sea = level < sea_ref[j : j + 1, :]
        raw = jnp.concatenate([inc_ref[h, pl.ds(j, nz, stride=8), :] for h in range(2)], axis=1)
        start = jnp.where(sea, raw * cell_ref[j : j + 1, :], 0.0)
        high, low = split(start)
        lifted = dot(lift3, jnp.concatenate([high, low, high], axis=0))
        for c in range(CHUNKS):
            first[c, 4 + j] = lifted[c * part : (c + 1) * part]
        mine = (lane128 >= HALO * j) & (lane128 < HALO * (j + 1))
        left = pltpu.roll(lifted[:, :128], HALO * j, 1) if j else lifted[:, :128]
        shift = (HALO * j - 112) % 128
        right = pltpu.roll(lifted[:, 128:], shift, 1) if shift else lifted[:, 128:]
        left_pack = jnp.where(mine, left, left_pack)
        right_pack = jnp.where(mine, right, right_pack)
    edge[0] = left_pack
    edge[1] = right_pack

    pl.semaphore_wait(barrier, 8)
    edge_copies = []
    for side, o in ((0, west), (1, east)):
        for slot, a in ((0, lat), (1, south), (2, north)):
            copy = pltpu.make_async_remote_copy(
                src_ref=edge.at[side],
                dst_ref=halo.at[1 - side, slot],
                send_sem=send_edge.at[side, slot],
                recv_sem=recv_edge.at[1 - side, slot],
                device_id={"lat": a, "lon": o},
                device_id_type=MESH,
            )
            copy.start()
            edge_copies.append(copy)

    def lat_copies(buffer, turn, c):
        copies = []
        for way, source, target, a in ((0, 4, 12, south), (1, 8, 0, north)):
            copy = pltpu.make_async_remote_copy(
                src_ref=buffer.at[c, pl.ds(source, 4)],
                dst_ref=buffer.at[c, pl.ds(target, 4)],
                send_sem=send_lat.at[turn, c, way],
                recv_sem=recv_lat.at[turn, c, way],
                device_id={"lat": a, "lon": lon},
                device_id_type=MESH,
            )
            copy.start()
            copies.append(copy)
        return copies

    first_copies = [lat_copies(first, 0, c) for c in range(CHUNKS)]

    column = lax.broadcasted_iota(jnp.int32, (lat_total, 256), 0)
    block = lax.broadcasted_iota(jnp.int32, (lat_total, 256), 1) // HALO
    row = 8 * lat + jnp.where(block < 12, block, block - 16)
    pick = jnp.where((column == row) & (column < lat_total - 1), 1.0, 0.0).astype(BF16)
    d_high, rest = diff_ref[...].astype(BF16), None
    rest = diff_ref[...] - d_high.astype(F32)
    d_mid, d_low = split(rest)
    packed_faces = dot(d_high, pick) + dot(d_mid, pick) + dot(d_low, pick)
    for m in range(15):
        lane = HALO * ((m - 4) % 16)
        faces_ref[m] = jnp.broadcast_to(packed_faces[:, lane : lane + 1], (nz, 128))

    inner = (
        lax.broadcasted_iota(jnp.int32, (128, 128), 0) - lax.broadcasted_iota(jnp.int32, (128, 128), 1)
    ).astype(F32)
    outer = (
        lax.broadcasted_iota(jnp.int32, (HALO, 128), 0) - lax.broadcasted_iota(jnp.int32, (HALO, 128), 1)
    ).astype(F32)
    w_high[...] = jnp.zeros_like(w_high)
    w_low[...] = jnp.zeros_like(w_low)
    for j in range(8):
        width = band_ref[8 * lat + j].astype(F32) + 1.0
        zscale[j : j + 1, :] = 1.0 / jnp.full((1, 256), 6.0 * (width * width) * (width * width), F32)
        for ref, a, b, c in zip(
            (w_high, w_low),
            split(band(inner, width)),
            split(band(outer - 16.0, width)),
            split(band(outer + 128.0, width)),
        ):
            ref[j, 0:128, 0:128] = a
            ref[j, 128:256, 128:256] = a
            ref[j, 112:128, 128:256] = b
            ref[j, 256 + HALO * j : 272 + HALO * j, 0:128] = b
            ref[j, 128:144, 0:128] = c
            ref[j, 384 + HALO * j : 400 + HALO * j, 128:256] = c

    for copy in edge_copies:
        copy.wait_recv()
    sides = []
    for side in range(2):
        other = jnp.where(lane128 < 64, halo[side, 1], halo[side, 2])
        field = jnp.concatenate([halo[side, 0], other], axis=1)
        for step in range(STEPS):
            flux = packed_faces * (pltpu.roll(field, 256 - HALO, 1) - field)
            field = field + (flux - pltpu.roll(flux, HALO, 1))
        sides.append(field[:, :128])
    halo_high, halo_low = split(jnp.concatenate(sides, axis=1))

    def rows_pass(buffer, c, store):
        def group(g, carry):
            at = pl.multiple_of(g * 8, 8)
            whole = pl.multiple_of(c * part + g * 8, 8)
            faces = [faces_ref[m, pl.ds(whole, 8), :] for m in range(15)]
            for half in range(2):
                lanes = slice(128 * half, 128 * half + 128)
                rows = [buffer[c, m, pl.ds(at, 8), lanes] for m in range(16)]
                for j, value in enumerate(diffuse(rows, faces)):
                    store[j, pl.ds(whole, 8), lanes] = value
            return carry

        lax.fori_loop(0, part // 8, group, 0)

    second_copies = []
    for c in range(CHUNKS):
        for copy in first_copies[c]:
            copy.wait_recv()
        rows_pass(first, c, mid)
        levels = slice(c * part, (c + 1) * part)
        for j in range(8):
            high, low = split(mid[j, levels, :])
            high = jnp.concatenate([high, halo_high[levels]], axis=1)
            low = jnp.concatenate([low, halo_low[levels]], axis=1)
            both = dot(jnp.concatenate([high, low], axis=0), w_high[j])
            total = both[:part] + both[part:] + dot(high, w_low[j])
            second[c, 4 + j] = total * zscale[j : j + 1, :]
        second_copies.append(lat_copies(second, 1, c))

    for c in range(CHUNKS):
        for copy in second_copies[c]:
            copy.wait_recv()
        rows_pass(second, c, fin)

    for j in range(8):
        high, low = split(fin[j])
        lowered = dot(lower3, jnp.concatenate([high, low, high], axis=0))
        sea = level < sea_ref[j : j + 1, :]
        result = jnp.where(sea, lowered * cell_ref[j : j + 1, :], 0.0)
        for h in range(2):
            out_ref[h, pl.ds(j, nz, stride=8), :] = result[:, 128 * h : 128 * h + 128]
    stores = [
        pltpu.make_async_copy(out_ref.at[h], out_hbm.at[:, pl.ds(128 * h, 128)], load_sem.at[h])
        for h in range(2)
    ]
    for store in stores:
        store.start()
    for copy in edge_copies:
        copy.wait_send()
    for group in first_copies + second_copies:
        for copy in group:
            copy.wait_send()
    for store in stores:
        store.wait()


def body(increment, sea_levels, cell_sigma, level_sigma, diffusivity, band_width, vertical_root):
    nz, rows, columns = increment.shape
    part = nz // CHUNKS
    vmem = pl.BlockSpec(memory_space=pltpu.VMEM)
    result = pl.pallas_call(
        kernel,
        out_shape=jax.ShapeDtypeStruct((nz * rows, columns), F32),
        in_specs=[
            pl.BlockSpec(memory_space=pltpu.SMEM),
            pl.BlockSpec(memory_space=pl.ANY),
            vmem, vmem, vmem, vmem, vmem,
        ],
        out_specs=pl.BlockSpec(memory_space=pl.ANY),
        scratch_shapes=[
            pltpu.VMEM((2, nz * rows, 128), F32),
            pltpu.VMEM((2, nz * rows, 128), F32),
            pltpu.VMEM((CHUNKS, 16, part, columns), F32),
            pltpu.VMEM((CHUNKS, 16, part, columns), F32),
            pltpu.VMEM((8, nz, columns), F32),
            pltpu.VMEM((8, nz, columns), F32),
            pltpu.VMEM((2, nz, 128), F32),
            pltpu.VMEM((2, 3, nz, 128), F32),
            pltpu.VMEM((15, nz, 128), F32),
            pltpu.VMEM((8, 512, 256), BF16),
            pltpu.VMEM((8, 512, 256), BF16),
            pltpu.VMEM((8, 256), F32),
            pltpu.SemaphoreType.DMA((2,)),
            pltpu.SemaphoreType.DMA((2, 3)),
            pltpu.SemaphoreType.DMA((2, 3)),
            pltpu.SemaphoreType.DMA((2, CHUNKS, 2)),
            pltpu.SemaphoreType.DMA((2, CHUNKS, 2)),
        ],
        compiler_params=pltpu.CompilerParams(collective_id=0, has_side_effects=True),
        name="covariance",
    )(
        band_width,
        increment.reshape(nz * rows, columns),
        sea_levels,
        cell_sigma,
        level_sigma.reshape(1, nz),
        diffusivity,
        vertical_root,
    )
    return result.reshape(nz, rows, columns)


def solution(mesh):
    return jax.shard_map(
        body,
        mesh=mesh,
        in_specs=(P(None, "lat", "lon"), P("lat", "lon"), P("lat", "lon"), P(), P(), P(), P()),
        out_specs=P(None, "lat", "lon"),
        check_vma=False,
    )
```

```python
import functools

import jax
import jax.numpy as jnp
from jax import lax
from jax.experimental import pallas as pl
from jax.experimental.pallas import tpu as pltpu
from jax.sharding import PartitionSpec as P

STEPS = 4
HALO = 16
CHUNKS = 2
F32 = jnp.float32
BF16 = jnp.bfloat16
MESH = pl.DeviceIdType.MESH


def split(value):
    high = value.astype(BF16)
    return high, (value - high.astype(F32)).astype(BF16)


def dot(left, right):
    return jnp.dot(left, right, preferred_element_type=F32)


def band(distance, width):
    u = jnp.maximum(2.0 * width - 1.0 - jnp.abs(distance), 0.0)
    v = jnp.maximum(u - width, 0.0)
    return u * (u + 1.0) * (u + 2.0) - 4.0 * (v * (v + 1.0) * (v + 2.0))


def diffuse(rows, faces):
    for step in range(STEPS):
        flux = [faces[step + m] * (rows[m + 1] - rows[m]) for m in range(len(rows) - 1)]
        rows = [rows[m] + (flux[m] - flux[m - 1]) for m in range(1, len(rows) - 1)]
    return rows


def kernel(
    band_hbm, inc_hbm, sea_hbm, cell_hbm, sigma_hbm, diff_hbm, root_hbm, out_ref,
    band_ref, sea_ref, cell_ref, sigma_ref, diff_ref, root_ref,
    inc_ref, first, second, mid, fin, edge, corner, halo, other, faces_ref, w_high, w_low, zscale,
    load_sem, send_edge, recv_edge, send_corner, recv_corner, send_lat, recv_lat,
):
    nz = root_ref.shape[0]
    lat_total = diff_ref.shape[1]
    part = nz // CHUNKS
    lat_count, lon_count = lax.axis_size("lat"), lax.axis_size("lon")
    lat, lon = lax.axis_index("lat"), lax.axis_index("lon")
    north, south = lax.rem(lat + 1, lat_count), lax.rem(lat + lat_count - 1, lat_count)
    east, west = lax.rem(lon + 1, lon_count), lax.rem(lon + lon_count - 1, lon_count)

    loads = [
        pltpu.make_async_copy(inc_hbm.at[:, pl.ds(128 * h, 128)], inc_ref.at[h], load_sem.at[h])
        for h in range(2)
    ]
    for i, (source, target) in enumerate(
        (
            (root_hbm, root_ref), (sigma_hbm, sigma_ref), (sea_hbm, sea_ref), (cell_hbm, cell_ref),
            (diff_hbm, diff_ref), (band_hbm, band_ref),
        )
    ):
        loads.append(pltpu.make_async_copy(source, target, load_sem.at[2 + i]))
    for load in loads:
        load.start()
    barrier = pltpu.get_barrier_semaphore()
    for a, o in (
        (north, lon), (south, lon), (lat, east), (lat, west),
        (north, east), (north, west), (south, east), (south, west),
    ):
        pl.semaphore_signal(barrier, inc=1, device_id={"lat": a, "lon": o}, device_id_type=MESH)

    loads[2].wait()
    loads[3].wait()
    lift = root_ref[...].T * sigma_ref[...]
    lift_high, lift_low = split(lift)
    lift3 = jnp.concatenate([lift_high, lift_high, lift_low], axis=1)
    lower_high, lower_low = split(lift.T)
    lower3 = jnp.concatenate([lower_high, lower_high, lower_low], axis=1)

    level = lax.broadcasted_iota(jnp.int32, (nz, 256), 0)
    lane128 = lax.broadcasted_iota(jnp.int32, (nz, 128), 1)

    for load in loads[4:6] + loads[:2]:
        load.wait()
    left_pack = jnp.zeros((nz, 128), F32)
    right_pack = jnp.zeros((nz, 128), F32)
    for j in range(8):
        sea = level < sea_ref[j : j + 1, :]
        raw = jnp.concatenate([inc_ref[h, pl.ds(j, nz, stride=8), :] for h in range(2)], axis=1)
        start = jnp.where(sea, raw * cell_ref[j : j + 1, :], 0.0)
        high, low = split(start)
        lifted = dot(lift3, jnp.concatenate([high, low, high], axis=0))
        for c in range(CHUNKS):
            first[c, 4 + j] = lifted[c * part : (c + 1) * part]
        mine = (lane128 >= HALO * j) & (lane128 < HALO * (j + 1))
        left = pltpu.roll(lifted[:, :128], HALO * j, 1) if j else lifted[:, :128]
        shift = (HALO * j - 112) % 128
        right = pltpu.roll(lifted[:, 128:], shift, 1) if shift else lifted[:, 128:]
        left_pack = jnp.where(mine, left, left_pack)
        right_pack = jnp.where(mine, right, right_pack)
    low_lanes = lane128[: nz // 2] < 64
    for side, pack in enumerate((left_pack, right_pack)):
        edge[side] = pack
        upper, turned = pack[: nz // 2], pltpu.roll(pack[nz // 2 :], 64, 1)
        corner[side, 0] = jnp.where(low_lanes, upper, turned)
        corner[side, 1] = jnp.where(low_lanes, turned, upper)

    def lat_copies(buffer, turn, c):
        copies = []
        for way, source, target, a in ((0, 4, 12, south), (1, 8, 0, north)):
            copy = pltpu.make_async_remote_copy(
                src_ref=buffer.at[c, pl.ds(source, 4)],
                dst_ref=buffer.at[c, pl.ds(target, 4)],
                send_sem=send_lat.at[turn, c, way],
                recv_sem=recv_lat.at[turn, c, way],
                device_id={"lat": a, "lon": lon},
                device_id_type=MESH,
            )
            copy.start()
            copies.append(copy)
        return copies

    pl.semaphore_wait(barrier, 8)
    edge_copies = []
    for side, o in ((0, west), (1, east)):
        copy = pltpu.make_async_remote_copy(
            src_ref=edge.at[side],
            dst_ref=halo.at[1 - side],
            send_sem=send_edge.at[side],
            recv_sem=recv_edge.at[1 - side],
            device_id={"lat": lat, "lon": o},
            device_id_type=MESH,
        )
        copy.start()
        edge_copies.append(copy)
    first_copies = [lat_copies(first, 0, 0)]
    for side, o in ((0, west), (1, east)):
        for way, a in ((0, south), (1, north)):
            copy = pltpu.make_async_remote_copy(
                src_ref=corner.at[side, way],
                dst_ref=other.at[1 - side, way],
                send_sem=send_corner.at[side, way],
                recv_sem=recv_corner.at[1 - side, way],
                device_id={"lat": a, "lon": o},
                device_id_type=MESH,
            )
            copy.start()
            edge_copies.append(copy)
    first_copies += [lat_copies(first, 0, c) for c in range(1, CHUNKS)]

    for load in loads[6:]:
        load.wait()
    column = lax.broadcasted_iota(jnp.int32, (lat_total, 256), 0)
    block = lax.broadcasted_iota(jnp.int32, (lat_total, 256), 1) // HALO
    row = 8 * lat + jnp.where(block < 12, block, block - 16)
    pick = jnp.where((column == row) & (column < lat_total - 1), 1.0, 0.0).astype(BF16)
    d_high, rest = diff_ref[...].astype(BF16), None
    rest = diff_ref[...] - d_high.astype(F32)
    d_mid, d_low = split(rest)
    packed_faces = dot(d_high, pick) + dot(d_mid, pick) + dot(d_low, pick)
    for m in range(15):
        lane = HALO * ((m - 4) % 16)
        faces_ref[m] = jnp.broadcast_to(packed_faces[:, lane : lane + 1], (nz, 128))

    inner = (
        lax.broadcasted_iota(jnp.int32, (128, 128), 0) - lax.broadcasted_iota(jnp.int32, (128, 128), 1)
    ).astype(F32)
    outer = (
        lax.broadcasted_iota(jnp.int32, (HALO, 128), 0) - lax.broadcasted_iota(jnp.int32, (HALO, 128), 1)
    ).astype(F32)
    w_high[...] = jnp.zeros_like(w_high)
    w_low[...] = jnp.zeros_like(w_low)
    for j in range(8):
        width = band_ref[8 * lat + j].astype(F32) + 1.0
        zscale[j : j + 1, :] = 1.0 / jnp.full((1, 256), 6.0 * (width * width) * (width * width), F32)
        for ref, a, b, c in zip(
            (w_high, w_low),
            split(band(inner, width)),
            split(band(outer - 16.0, width)),
            split(band(outer + 128.0, width)),
        ):
            ref[j, 0:128, 0:128] = a
            ref[j, 128:256, 128:256] = a
            ref[j, 112:128, 128:256] = b
            ref[j, 256 + HALO * j : 272 + HALO * j, 0:128] = b
            ref[j, 128:144, 0:128] = c
            ref[j, 384 + HALO * j : 400 + HALO * j, 128:256] = c

    def halo_pass():
        for copy in edge_copies:
            copy.wait_recv()
        sides = []
        for side in range(2):
            above, below = other[side, 0], other[side, 1]
            far = jnp.concatenate(
                [
                    jnp.where(low_lanes, above, below),
                    pltpu.roll(jnp.where(low_lanes, below, above), 64, 1),
                ],
                axis=0,
            )
            field = jnp.concatenate([halo[side], far], axis=1)
            for step in range(STEPS):
                flux = packed_faces * (pltpu.roll(field, 256 - HALO, 1) - field)
                field = field + (flux - pltpu.roll(flux, HALO, 1))
            sides.append(field[:, :128])
        return split(jnp.concatenate(sides, axis=1))

    def rows_pass(buffer, c, store):
        def group(g, carry):
            at = pl.multiple_of(g * 8, 8)
            whole = pl.multiple_of(c * part + g * 8, 8)
            faces = [faces_ref[m, pl.ds(whole, 8), :] for m in range(15)]
            for half in range(2):
                lanes = slice(128 * half, 128 * half + 128)
                rows = [buffer[c, m, pl.ds(at, 8), lanes] for m in range(16)]
                for j, value in enumerate(diffuse(rows, faces)):
                    store[j, pl.ds(whole, 8), lanes] = value
            return carry

        lax.fori_loop(0, part // 8, group, 0)

    second_copies = []
    for c in range(CHUNKS):
        for copy in first_copies[c]:
            copy.wait_recv()
        rows_pass(first, c, mid)
        if c == 0:
            halo_high, halo_low = halo_pass()
        levels = slice(c * part, (c + 1) * part)
        for j in range(8):
            high, low = split(mid[j, levels, :])
            high = jnp.concatenate([high, halo_high[levels]], axis=1)
            low = jnp.concatenate([low, halo_low[levels]], axis=1)
            both = dot(jnp.concatenate([high, low], axis=0), w_high[j])
            total = both[:part] + both[part:] + dot(high, w_low[j])
            second[c, 4 + j] = total * zscale[j : j + 1, :]
        second_copies.append(lat_copies(second, 1, c))

    for c in range(CHUNKS):
        for copy in second_copies[c]:
            copy.wait_recv()
        rows_pass(second, c, fin)

    for j in range(8):
        high, low = split(fin[j])
        lowered = dot(lower3, jnp.concatenate([high, low, high], axis=0))
        sea = level < sea_ref[j : j + 1, :]
        result = jnp.where(sea, lowered * cell_ref[j : j + 1, :], 0.0)
        for h in range(2):
            out_ref[pl.ds(8 * h + j, nz, stride=16), :] = result[:, 128 * h : 128 * h + 128]
    for copy in edge_copies:
        copy.wait_send()
    for group in first_copies + second_copies:
        for copy in group:
            copy.wait_send()


def body(increment, sea_levels, cell_sigma, level_sigma, diffusivity, band_width, vertical_root):
    nz, rows, columns = increment.shape
    part = nz // CHUNKS
    result = pl.pallas_call(
        kernel,
        out_shape=jax.ShapeDtypeStruct((2 * nz * rows, 128), F32),
        in_specs=[
            pl.BlockSpec(memory_space=pl.ANY)
        ]
        * 7,
        out_specs=pl.BlockSpec(memory_space=pltpu.VMEM),
        scratch_shapes=[
            pltpu.SMEM(band_width.shape, jnp.int32),
            pltpu.VMEM(sea_levels.shape, jnp.int32),
            pltpu.VMEM(cell_sigma.shape, F32),
            pltpu.VMEM((1, nz), F32),
            pltpu.VMEM(diffusivity.shape, F32),
            pltpu.VMEM(vertical_root.shape, F32),
            pltpu.VMEM((2, nz * rows, 128), F32),
            pltpu.VMEM((CHUNKS, 16, part, columns), F32),
            pltpu.VMEM((CHUNKS, 16, part, columns), F32),
            pltpu.VMEM((8, nz, columns), F32),
            pltpu.VMEM((8, nz, columns), F32),
            pltpu.VMEM((2, nz, 128), F32),
            pltpu.VMEM((2, 2, nz // 2, 128), F32),
            pltpu.VMEM((2, nz, 128), F32),
            pltpu.VMEM((2, 2, nz // 2, 128), F32),
            pltpu.VMEM((15, nz, 128), F32),
            pltpu.VMEM((8, 512, 256), BF16),
            pltpu.VMEM((8, 512, 256), BF16),
            pltpu.VMEM((8, 256), F32),
            pltpu.SemaphoreType.DMA((8,)),
            pltpu.SemaphoreType.DMA((2,)),
            pltpu.SemaphoreType.DMA((2,)),
            pltpu.SemaphoreType.DMA((2, 2)),
            pltpu.SemaphoreType.DMA((2, 2)),
            pltpu.SemaphoreType.DMA((2, CHUNKS, 2)),
            pltpu.SemaphoreType.DMA((2, CHUNKS, 2)),
        ],
        compiler_params=pltpu.CompilerParams(collective_id=0, has_side_effects=True, vmem_limit_bytes=24 * 2**20),
        name="covariance",
    )(*(pltpu.with_memory_space_constraint(x, pltpu.HBM) for x in (
        band_width,
        increment.reshape(nz * rows, columns),
        sea_levels,
        cell_sigma,
        level_sigma.reshape(1, nz),
        diffusivity,
        vertical_root,
    )))
    result = result.reshape(nz, 2, rows, 128).transpose(0, 2, 1, 3)
    return result.reshape(nz, rows, columns)


def solution(mesh):
    return jax.shard_map(
        body,
        mesh=mesh,
        in_specs=(P(None, "lat", "lon"), P("lat", "lon"), P("lat", "lon"), P(), P(), P(), P()),
        out_specs=P(None, "lat", "lon"),
        check_vma=False,
    )
```

```python
import functools

import jax
import jax.numpy as jnp
from jax import lax
from jax.experimental import pallas as pl
from jax.experimental.pallas import tpu as pltpu
from jax.sharding import PartitionSpec as P

STEPS = 4
HALO = 16
CHUNKS = 2
F32 = jnp.float32
BF16 = jnp.bfloat16
MESH = pl.DeviceIdType.MESH


def split(value):
    high = value.astype(BF16)
    return high, (value - high.astype(F32)).astype(BF16)


def dot(left, right):
    return jnp.dot(left, right, preferred_element_type=F32)


def band(distance, width):
    u = jnp.maximum(2.0 * width - 1.0 - jnp.abs(distance), 0.0)
    v = jnp.maximum(u - width, 0.0)
    return u * (u + 1.0) * (u + 2.0) - 4.0 * (v * (v + 1.0) * (v + 2.0))


def diffuse(rows, faces):
    for step in range(STEPS):
        flux = [faces[step + m] * (rows[m + 1] - rows[m]) for m in range(len(rows) - 1)]
        rows = [rows[m] + (flux[m] - flux[m - 1]) for m in range(1, len(rows) - 1)]
    return rows


def kernel(
    band_hbm, inc_hbm, sea_hbm, cell_hbm, sigma_hbm, diff_hbm, root_hbm, out_ref,
    band_ref, sea_ref, cell_ref, sigma_ref, diff_ref, root_ref,
    inc_ref, first, second, mid, fin, edge, halo, other, faces_ref, w_high, w_low, zscale,
    load_sem, send_edge, recv_edge, send_corner, recv_corner, send_lat, recv_lat,
):
    nz = root_ref.shape[0]
    lat_total = diff_ref.shape[1]
    part = nz // CHUNKS
    lat_count, lon_count = lax.axis_size("lat"), lax.axis_size("lon")
    lat, lon = lax.axis_index("lat"), lax.axis_index("lon")
    north, south = lax.rem(lat + 1, lat_count), lax.rem(lat + lat_count - 1, lat_count)
    east, west = lax.rem(lon + 1, lon_count), lax.rem(lon + lon_count - 1, lon_count)

    loads = [
        pltpu.make_async_copy(inc_hbm.at[:, pl.ds(128 * h, 128)], inc_ref.at[h], load_sem.at[h])
        for h in range(2)
    ]
    for i, (source, target) in enumerate(
        (
            (root_hbm, root_ref), (sigma_hbm, sigma_ref), (sea_hbm, sea_ref), (cell_hbm, cell_ref),
            (diff_hbm, diff_ref), (band_hbm, band_ref),
        )
    ):
        loads.append(pltpu.make_async_copy(source, target, load_sem.at[2 + i]))
    for load in loads:
        load.start()
    barrier = pltpu.get_barrier_semaphore()
    for a, o in (
        (north, lon), (south, lon), (lat, east), (lat, west),
        (north, east), (north, west), (south, east), (south, west),
    ):
        pl.semaphore_signal(barrier, inc=1, device_id={"lat": a, "lon": o}, device_id_type=MESH)

    loads[2].wait()
    loads[3].wait()
    lift = root_ref[...].T * sigma_ref[...]
    lift_high, lift_low = split(lift)
    lift3 = jnp.concatenate([lift_high, lift_high, lift_low], axis=1)
    lower_high, lower_low = split(lift.T)
    lower3 = jnp.concatenate([lower_high, lower_high, lower_low], axis=1)

    level = lax.broadcasted_iota(jnp.int32, (nz, 256), 0)
    lane128 = lax.broadcasted_iota(jnp.int32, (nz, 128), 1)

    for load in loads[4:6] + loads[:2]:
        load.wait()
    left_pack = jnp.zeros((nz, 128), F32)
    right_pack = jnp.zeros((nz, 128), F32)
    for j in range(8):
        sea = level < sea_ref[j : j + 1, :]
        raw = jnp.concatenate([inc_ref[h, pl.ds(j, nz, stride=8), :] for h in range(2)], axis=1)
        start = jnp.where(sea, raw * cell_ref[j : j + 1, :], 0.0)
        high, low = split(start)
        lifted = dot(lift3, jnp.concatenate([high, low, high], axis=0))
        for c in range(CHUNKS):
            first[c, 8 + j] = lifted[c * part : (c + 1) * part]
        mine = (lane128 >= HALO * j) & (lane128 < HALO * (j + 1))
        left = pltpu.roll(lifted[:, :128], HALO * j, 1) if j else lifted[:, :128]
        shift = (HALO * j - 112) % 128
        right = pltpu.roll(lifted[:, 128:], shift, 1) if shift else lifted[:, 128:]
        left_pack = jnp.where(mine, left, left_pack)
        right_pack = jnp.where(mine, right, right_pack)
    edge[0] = left_pack
    edge[1] = right_pack

    def lat_copies(c):
        copies = []
        for way, target, a in ((0, 0, north), (1, 16, south)):
            copy = pltpu.make_async_remote_copy(
                src_ref=first.at[c, pl.ds(8, 8)],
                dst_ref=first.at[c, pl.ds(target, 8)],
                send_sem=send_lat.at[c, way],
                recv_sem=recv_lat.at[c, way],
                device_id={"lat": a, "lon": lon},
                device_id_type=MESH,
            )
            copy.start()
            copies.append(copy)
        return copies

    pl.semaphore_wait(barrier, 8)
    edge_copies = []
    for side, o in ((0, west), (1, east)):
        copy = pltpu.make_async_remote_copy(
            src_ref=edge.at[side],
            dst_ref=halo.at[1 - side],
            send_sem=send_edge.at[side],
            recv_sem=recv_edge.at[1 - side],
            device_id={"lat": lat, "lon": o},
            device_id_type=MESH,
        )
        copy.start()
        edge_copies.append(copy)
    first_copies = [lat_copies(0)]
    for side, o in ((0, west), (1, east)):
        for way, a in ((0, south), (1, north)):
            copy = pltpu.make_async_remote_copy(
                src_ref=edge.at[side],
                dst_ref=other.at[1 - side, way],
                send_sem=send_corner.at[side, way],
                recv_sem=recv_corner.at[1 - side, way],
                device_id={"lat": a, "lon": o},
                device_id_type=MESH,
            )
            copy.start()
            edge_copies.append(copy)
    first_copies += [lat_copies(c) for c in range(1, CHUNKS)]

    for load in loads[6:]:
        load.wait()
    column = lax.broadcasted_iota(jnp.int32, (lat_total, 384), 0)
    block = lax.broadcasted_iota(jnp.int32, (lat_total, 384), 1) // HALO
    row = 8 * lat + jnp.where(block < 16, block, block - 24)
    pick = jnp.where((column == row) & (column < lat_total - 1), 1.0, 0.0).astype(BF16)
    d_high, rest = diff_ref[...].astype(BF16), None
    rest = diff_ref[...] - d_high.astype(F32)
    d_mid, d_low = split(rest)
    packed_faces = dot(d_high, pick) + dot(d_mid, pick) + dot(d_low, pick)
    for m in range(23):
        lane = HALO * ((m - 8) % 24)
        faces_ref[m] = jnp.broadcast_to(packed_faces[:, lane : lane + 1], (nz, 128))

    inner = (
        lax.broadcasted_iota(jnp.int32, (128, 128), 0) - lax.broadcasted_iota(jnp.int32, (128, 128), 1)
    ).astype(F32)
    outer = (
        lax.broadcasted_iota(jnp.int32, (HALO, 128), 0) - lax.broadcasted_iota(jnp.int32, (HALO, 128), 1)
    ).astype(F32)
    w_high[...] = jnp.zeros_like(w_high)
    w_low[...] = jnp.zeros_like(w_low)
    for q in range(16):
        j = (q - 4) % 8
        width = band_ref[lax.rem(8 * lat + (q - 4 + lat_total), lat_total)].astype(F32) + 1.0
        zscale[q : q + 1, :] = 1.0 / jnp.full((1, 256), 6.0 * (width * width) * (width * width), F32)
        for ref, a, b, c in zip(
            (w_high, w_low),
            split(band(inner, width)),
            split(band(outer - 16.0, width)),
            split(band(outer + 128.0, width)),
        ):
            ref[q, 0:128, 0:128] = a
            ref[q, 128:256, 128:256] = a
            ref[q, 112:128, 128:256] = b
            ref[q, 256 + HALO * j : 272 + HALO * j, 0:128] = b
            ref[q, 128:144, 0:128] = c
            ref[q, 384 + HALO * j : 400 + HALO * j, 128:256] = c

    def halo_pass():
        for copy in edge_copies:
            copy.wait_recv()
        sides = []
        for side in range(2):
            field = jnp.concatenate([halo[side], other[side, 0], other[side, 1]], axis=1)
            for step in range(STEPS):
                flux = packed_faces * (pltpu.roll(field, 384 - HALO, 1) - field)
                field = field + (flux - pltpu.roll(flux, HALO, 1))
            sides.append(field)
        return [
            split(jnp.concatenate([field[:, 128 * v : 128 * v + 128] for field in sides], axis=1))
            for v in range(3)
        ]

    def rows_pass(buffer, c, base, face, store, offset):
        def group(g, carry):
            at = pl.multiple_of(g * 8, 8)
            whole = pl.multiple_of(c * part + g * 8, 8)
            faces = [faces_ref[face + m, pl.ds(whole, 8), :] for m in range(15)]
            for half in range(2):
                lanes = slice(128 * half, 128 * half + 128)
                rows = [buffer[c, base + m, pl.ds(at, 8), lanes] for m in range(16)]
                for j, value in enumerate(diffuse(rows, faces)):
                    store[offset + j, pl.ds(whole, 8), lanes] = value
            return carry

        lax.fori_loop(0, part // 8, group, 0)

    def zonal(c, start):
        levels = slice(c * part, (c + 1) * part)
        for q in range(start, start + 8):
            halo_high, halo_low = halos[0 if 4 <= q < 12 else 1 if q >= 12 else 2]
            high, low = split(mid[q, levels, :])
            high = jnp.concatenate([high, halo_high[levels]], axis=1)
            low = jnp.concatenate([low, halo_low[levels]], axis=1)
            both = dot(jnp.concatenate([high, low], axis=0), w_high[q])
            total = both[:part] + both[part:] + dot(high, w_low[q])
            second[c, q] = total * zscale[q : q + 1, :]

    for c in range(CHUNKS):
        first_copies[c][1].wait_recv()
        rows_pass(first, c, 8, 8, mid, 8)
    halos = halo_pass()
    for c in range(CHUNKS):
        zonal(c, 8)
    for c in range(CHUNKS):
        first_copies[c][0].wait_recv()
        rows_pass(first, c, 0, 0, mid, 0)
        zonal(c, 0)
        rows_pass(second, c, 0, 4, fin, 0)

    for j in range(8):
        high, low = split(fin[j])
        lowered = dot(lower3, jnp.concatenate([high, low, high], axis=0))
        sea = level < sea_ref[j : j + 1, :]
        result = jnp.where(sea, lowered * cell_ref[j : j + 1, :], 0.0)
        for h in range(2):
            out_ref[pl.ds(8 * h + j, nz, stride=16), :] = result[:, 128 * h : 128 * h + 128]
    for copy in edge_copies:
        copy.wait_send()
    for group in first_copies:
        for copy in group:
            copy.wait_send()


def body(increment, sea_levels, cell_sigma, level_sigma, diffusivity, band_width, vertical_root):
    nz, rows, columns = increment.shape
    part = nz // CHUNKS
    result = pl.pallas_call(
        kernel,
        out_shape=jax.ShapeDtypeStruct((2 * nz * rows, 128), F32),
        in_specs=[
            pl.BlockSpec(memory_space=pl.ANY)
        ]
        * 7,
        out_specs=pl.BlockSpec(memory_space=pltpu.VMEM),
        scratch_shapes=[
            pltpu.SMEM(band_width.shape, jnp.int32),
            pltpu.VMEM(sea_levels.shape, jnp.int32),
            pltpu.VMEM(cell_sigma.shape, F32),
            pltpu.VMEM((1, nz), F32),
            pltpu.VMEM(diffusivity.shape, F32),
            pltpu.VMEM(vertical_root.shape, F32),
            pltpu.VMEM((2, nz * rows, 128), F32),
            pltpu.VMEM((CHUNKS, 24, part, columns), F32),
            pltpu.VMEM((CHUNKS, 16, part, columns), F32),
            pltpu.VMEM((16, nz, columns), F32),
            pltpu.VMEM((8, nz, columns), F32),
            pltpu.VMEM((2, nz, 128), F32),
            pltpu.VMEM((2, nz, 128), F32),
            pltpu.VMEM((2, 2, nz, 128), F32),
            pltpu.VMEM((23, nz, 128), F32),
            pltpu.VMEM((16, 512, 256), BF16),
            pltpu.VMEM((16, 512, 256), BF16),
            pltpu.VMEM((16, 256), F32),
            pltpu.SemaphoreType.DMA((8,)),
            pltpu.SemaphoreType.DMA((2,)),
            pltpu.SemaphoreType.DMA((2,)),
            pltpu.SemaphoreType.DMA((2, 2)),
            pltpu.SemaphoreType.DMA((2, 2)),
            pltpu.SemaphoreType.DMA((CHUNKS, 2)),
            pltpu.SemaphoreType.DMA((CHUNKS, 2)),
        ],
        compiler_params=pltpu.CompilerParams(collective_id=0, has_side_effects=True, vmem_limit_bytes=24 * 2**20),
        name="covariance",
    )(*(pltpu.with_memory_space_constraint(x, pltpu.HBM) for x in (
        band_width,
        increment.reshape(nz * rows, columns),
        sea_levels,
        cell_sigma,
        level_sigma.reshape(1, nz),
        diffusivity,
        vertical_root,
    )))
    result = result.reshape(nz, 2, rows, 128).transpose(0, 2, 1, 3)
    return result.reshape(nz, rows, columns)


def solution(mesh):
    return jax.shard_map(
        body,
        mesh=mesh,
        in_specs=(P(None, "lat", "lon"), P("lat", "lon"), P("lat", "lon"), P(), P(), P(), P()),
        out_specs=P(None, "lat", "lon"),
        check_vma=False,
    )
```

```python
import functools

import jax
import jax.numpy as jnp
from jax import lax
from jax.experimental import pallas as pl
from jax.experimental.pallas import tpu as pltpu
from jax.sharding import PartitionSpec as P

STEPS = 4
HALO = 16
CHUNKS = 2
F32 = jnp.float32
BF16 = jnp.bfloat16
MESH = pl.DeviceIdType.MESH


def split(value):
    high = value.astype(BF16)
    return high, (value - high.astype(F32)).astype(BF16)


def dot(left, right):
    return jnp.dot(left, right, preferred_element_type=F32)


def band(distance, width):
    u = jnp.maximum(2.0 * width - 1.0 - jnp.abs(distance), 0.0)
    v = jnp.maximum(u - width, 0.0)
    return u * (u + 1.0) * (u + 2.0) - 4.0 * (v * (v + 1.0) * (v + 2.0))


def diffuse(rows, faces):
    for step in range(STEPS):
        flux = [faces[step + m] * (rows[m + 1] - rows[m]) for m in range(len(rows) - 1)]
        rows = [rows[m] + (flux[m] - flux[m - 1]) for m in range(1, len(rows) - 1)]
    return rows


def kernel(
    band_hbm, inc_hbm, sea_hbm, cell_hbm, sigma_hbm, diff_hbm, root_hbm, out_ref,
    band_ref, sea_ref, cell_ref, sigma_ref, diff_ref, root_ref,
    inc_ref, first, second, mid, fin, edge, halo, other, faces_ref, w_high, w_low, zscale, halos,
    load_sem, send_edge, recv_edge, send_corner, recv_corner, send_lat, recv_lat,
):
    nz = root_ref.shape[0]
    lat_total = diff_ref.shape[1]
    part = nz // CHUNKS
    lat_count, lon_count = lax.axis_size("lat"), lax.axis_size("lon")
    lat, lon = lax.axis_index("lat"), lax.axis_index("lon")
    north, south = lax.rem(lat + 1, lat_count), lax.rem(lat + lat_count - 1, lat_count)
    east, west = lax.rem(lon + 1, lon_count), lax.rem(lon + lon_count - 1, lon_count)

    loads = [
        pltpu.make_async_copy(inc_hbm.at[:, pl.ds(128 * h, 128)], inc_ref.at[h], load_sem.at[h])
        for h in range(2)
    ]
    for i, (source, target) in enumerate(
        (
            (root_hbm, root_ref), (sigma_hbm, sigma_ref), (sea_hbm, sea_ref), (cell_hbm, cell_ref),
            (diff_hbm, diff_ref), (band_hbm, band_ref),
        )
    ):
        loads.append(pltpu.make_async_copy(source, target, load_sem.at[2 + i]))
    for load in loads:
        load.start()
    has_south, has_north = lat > 0, lat < lat_count - 1
    barrier = pltpu.get_barrier_semaphore()

    def greet(a, columns):
        for o in columns:
            pl.semaphore_signal(barrier, inc=1, device_id={"lat": a, "lon": o}, device_id_type=MESH)

    greet(lat, (east, west))
    pl.when(has_south)(lambda: greet(south, (lon, east, west)))
    pl.when(has_north)(lambda: greet(north, (lon, east, west)))

    loads[2].wait()
    loads[3].wait()
    lift = root_ref[...].T * sigma_ref[...]
    lift_high, lift_low = split(lift)
    lift3 = jnp.concatenate([lift_high, lift_high, lift_low], axis=1)
    lower_high, lower_low = split(lift.T)
    lower3 = jnp.concatenate([lower_high, lower_high, lower_low], axis=1)

    level = lax.broadcasted_iota(jnp.int32, (nz, 256), 0)
    lane128 = lax.broadcasted_iota(jnp.int32, (nz, 128), 1)

    for load in loads[4:6] + loads[:2]:
        load.wait()
    left_pack = jnp.zeros((nz, 128), F32)
    right_pack = jnp.zeros((nz, 128), F32)
    for j in range(8):
        sea = level < sea_ref[j : j + 1, :]
        raw = jnp.concatenate([inc_ref[h, pl.ds(j, nz, stride=8), :] for h in range(2)], axis=1)
        start = jnp.where(sea, raw * cell_ref[j : j + 1, :], 0.0)
        high, low = split(start)
        lifted = dot(lift3, jnp.concatenate([high, low, high], axis=0))
        for c in range(CHUNKS):
            first[c, 8 + j] = lifted[c * part : (c + 1) * part]
        mine = (lane128 >= HALO * j) & (lane128 < HALO * (j + 1))
        left = pltpu.roll(lifted[:, :128], HALO * j, 1) if j else lifted[:, :128]
        shift = (HALO * j - 112) % 128
        right = pltpu.roll(lifted[:, 128:], shift, 1) if shift else lifted[:, 128:]
        left_pack = jnp.where(mine, left, left_pack)
        right_pack = jnp.where(mine, right, right_pack)
    edge[0] = left_pack
    edge[1] = right_pack

    @pl.when(jnp.logical_not(has_south))
    def _():
        first[:, 0:8] = jnp.zeros_like(first[:, 0:8])
        other[:, 1] = jnp.zeros_like(other[:, 1])

    @pl.when(jnp.logical_not(has_north))
    def _():
        first[:, 16:24] = jnp.zeros_like(first[:, 16:24])
        other[:, 0] = jnp.zeros_like(other[:, 0])

    def lat_copy(c, way, a):
        return pltpu.make_async_remote_copy(
            src_ref=first.at[c, pl.ds(8, 8)],
            dst_ref=first.at[c, pl.ds(16 * way, 8)],
            send_sem=send_lat.at[c, way],
            recv_sem=recv_lat.at[c, way],
            device_id={"lat": a, "lon": lon},
            device_id_type=MESH,
        )

    def send_rows(c):
        pl.when(has_north)(lambda: lat_copy(c, 0, north).start())
        pl.when(has_south)(lambda: lat_copy(c, 1, south).start())

    inside = has_south.astype(jnp.int32) + has_north.astype(jnp.int32)
    pl.semaphore_wait(barrier, 2 + 3 * inside)
    edge_copies = []
    for side, o in ((0, west), (1, east)):
        copy = pltpu.make_async_remote_copy(
            src_ref=edge.at[side],
            dst_ref=halo.at[1 - side],
            send_sem=send_edge.at[side],
            recv_sem=recv_edge.at[1 - side],
            device_id={"lat": lat, "lon": o},
            device_id_type=MESH,
        )
        copy.start()
        edge_copies.append(copy)
    send_rows(0)
    def corner_copies(way, a):
        return [
            pltpu.make_async_remote_copy(
                src_ref=edge.at[side],
                dst_ref=other.at[1 - side, way],
                send_sem=send_corner.at[side, way],
                recv_sem=recv_corner.at[1 - side, way],
                device_id={"lat": a, "lon": o},
                device_id_type=MESH,
            )
            for side, o in ((0, west), (1, east))
        ]

    def each(copies, action):
        for copy in copies:
            getattr(copy, action)()

    pl.when(has_south)(lambda: each(corner_copies(0, south), "start"))
    pl.when(has_north)(lambda: each(corner_copies(1, north), "start"))
    for c in range(1, CHUNKS):
        send_rows(c)

    for load in loads[6:]:
        load.wait()
    column = lax.broadcasted_iota(jnp.int32, (lat_total, 384), 0)
    block = lax.broadcasted_iota(jnp.int32, (lat_total, 384), 1) // HALO
    row = 8 * lat + jnp.where(block < 16, block, block - 24)
    pick = jnp.where((column == row) & (column < lat_total - 1), 1.0, 0.0).astype(BF16)
    d_high, rest = diff_ref[...].astype(BF16), None
    rest = diff_ref[...] - d_high.astype(F32)
    d_mid, d_low = split(rest)
    packed_faces = dot(d_high, pick) + dot(d_mid, pick) + dot(d_low, pick)
    for m in range(23):
        lane = HALO * ((m - 8) % 24)
        faces_ref[m] = jnp.broadcast_to(packed_faces[:, lane : lane + 1], (nz, 128))

    inner = (
        lax.broadcasted_iota(jnp.int32, (128, 128), 0) - lax.broadcasted_iota(jnp.int32, (128, 128), 1)
    ).astype(F32)
    outer = (
        lax.broadcasted_iota(jnp.int32, (HALO, 128), 0) - lax.broadcasted_iota(jnp.int32, (HALO, 128), 1)
    ).astype(F32)
    w_high[...] = jnp.zeros_like(w_high)
    w_low[...] = jnp.zeros_like(w_low)
    for q in range(16):
        j = (q - 4) % 8
        width = band_ref[lax.rem(8 * lat + (q - 4 + lat_total), lat_total)].astype(F32) + 1.0
        zscale[q] = 1.0 / jnp.full((1, 256), 6.0 * (width * width) * (width * width), F32)
        for ref, a, b, c in zip(
            (w_high, w_low),
            split(band(inner, width)),
            split(band(outer - 16.0, width)),
            split(band(outer + 128.0, width)),
        ):
            ref[q, 0:128, 0:128] = a
            ref[q, 128:256, 128:256] = a
            ref[q, 112:128, 128:256] = b
            ref[q, 256 + HALO * j : 272 + HALO * j, 0:128] = b
            ref[q, 128:144, 0:128] = c
            ref[q, 384 + HALO * j : 400 + HALO * j, 128:256] = c

    def halo_pass():
        each(edge_copies, "wait_recv")
        pl.when(has_north)(lambda: each(corner_copies(0, south), "wait_recv"))
        pl.when(has_south)(lambda: each(corner_copies(1, north), "wait_recv"))
        sides = []
        for side in range(2):
            field = jnp.concatenate([halo[side], other[side, 0], other[side, 1]], axis=1)
            for step in range(STEPS):
                flux = packed_faces * (pltpu.roll(field, 384 - HALO, 1) - field)
                field = field + (flux - pltpu.roll(flux, HALO, 1))
            sides.append(field)
        for v in range(3):
            halos[v, 0], halos[v, 1] = split(
                jnp.concatenate([field[:, 128 * v : 128 * v + 128] for field in sides], axis=1)
            )

    def rows_pass(buffer, c, base, face, store, offset):
        def group(g, carry):
            at = pl.multiple_of(g * 8, 8)
            whole = pl.multiple_of(c * part + g * 8, 8)
            faces = [faces_ref[face + m, pl.ds(whole, 8), :] for m in range(15)]
            for half in range(2):
                lanes = slice(128 * half, 128 * half + 128)
                rows = [buffer[c, base + m, pl.ds(at, 8), lanes] for m in range(16)]
                for j, value in enumerate(diffuse(rows, faces)):
                    store[offset + j, pl.ds(whole, 8), lanes] = value
            return carry

        lax.fori_loop(0, part // 8, group, 0)

    def zonal(c, half):
        levels = slice(c * part, (c + 1) * part)
        for i in range(8):
            q = 8 * half + i
            group = 2 - 2 * half if i < 4 else half
            high, low = split(mid[q, levels, :])
            high = jnp.concatenate([high, halos[group, 0, levels, :]], axis=1)
            low = jnp.concatenate([low, halos[group, 1, levels, :]], axis=1)
            both = dot(jnp.concatenate([high, low], axis=0), w_high[q])
            total = both[:part] + both[part:] + dot(high, w_low[q])
            second[c, q] = total * zscale[q]

    def receive(c, half):
        there = jnp.where(half == 0, lat, lat_count - 1 - lat) > 0
        pl.when(there)(lambda: lat_copy(c, half, north).wait_recv())
        rows_pass(first, c, 8 * half, 8 * half, mid, 8 * half)

    late = lax.rem(lat, 2)
    early = 1 - late
    for c in range(CHUNKS):
        receive(c, early)
    halo_pass()
    for c in range(CHUNKS):
        zonal(c, early)
    for c in range(CHUNKS):
        receive(c, late)
        zonal(c, late)
        rows_pass(second, c, 0, 4, fin, 0)

    for j in range(8):
        high, low = split(fin[j])
        lowered = dot(lower3, jnp.concatenate([high, low, high], axis=0))
        sea = level < sea_ref[j : j + 1, :]
        result = jnp.where(sea, lowered * cell_ref[j : j + 1, :], 0.0)
        for h in range(2):
            out_ref[pl.ds(8 * h + j, nz, stride=16), :] = result[:, 128 * h : 128 * h + 128]
    each(edge_copies, "wait_send")

    def sent(corner_way, a, way):
        each(corner_copies(corner_way, a), "wait_send")
        each([lat_copy(c, way, a) for c in range(CHUNKS)], "wait_send")

    pl.when(has_south)(lambda: sent(0, south, 1))
    pl.when(has_north)(lambda: sent(1, north, 0))


def body(increment, sea_levels, cell_sigma, level_sigma, diffusivity, band_width, vertical_root):
    nz, rows, columns = increment.shape
    part = nz // CHUNKS
    result = pl.pallas_call(
        kernel,
        out_shape=jax.ShapeDtypeStruct((2 * nz * rows, 128), F32),
        in_specs=[
            pl.BlockSpec(memory_space=pl.ANY)
        ]
        * 7,
        out_specs=pl.BlockSpec(memory_space=pltpu.VMEM),
        scratch_shapes=[
            pltpu.SMEM(band_width.shape, jnp.int32),
            pltpu.VMEM(sea_levels.shape, jnp.int32),
            pltpu.VMEM(cell_sigma.shape, F32),
            pltpu.VMEM((1, nz), F32),
            pltpu.VMEM(diffusivity.shape, F32),
            pltpu.VMEM(vertical_root.shape, F32),
            pltpu.VMEM((2, nz * rows, 128), F32),
            pltpu.VMEM((CHUNKS, 24, part, columns), F32),
            pltpu.VMEM((CHUNKS, 16, part, columns), F32),
            pltpu.VMEM((16, nz, columns), F32),
            pltpu.VMEM((8, nz, columns), F32),
            pltpu.VMEM((2, nz, 128), F32),
            pltpu.VMEM((2, nz, 128), F32),
            pltpu.VMEM((2, 2, nz, 128), F32),
            pltpu.VMEM((23, nz, 128), F32),
            pltpu.VMEM((16, 512, 256), BF16),
            pltpu.VMEM((16, 512, 256), BF16),
            pltpu.VMEM((16, 1, 256), F32),
            pltpu.VMEM((3, 2, nz, columns), BF16),
            pltpu.SemaphoreType.DMA((8,)),
            pltpu.SemaphoreType.DMA((2,)),
            pltpu.SemaphoreType.DMA((2,)),
            pltpu.SemaphoreType.DMA((2, 2)),
            pltpu.SemaphoreType.DMA((2, 2)),
            pltpu.SemaphoreType.DMA((CHUNKS, 2)),
            pltpu.SemaphoreType.DMA((CHUNKS, 2)),
        ],
        compiler_params=pltpu.CompilerParams(collective_id=0, has_side_effects=True, vmem_limit_bytes=24 * 2**20),
        name="covariance",
    )(*(pltpu.with_memory_space_constraint(x, pltpu.HBM) for x in (
        band_width,
        increment.reshape(nz * rows, columns),
        sea_levels,
        cell_sigma,
        level_sigma.reshape(1, nz),
        diffusivity,
        vertical_root,
    )))
    result = result.reshape(nz, 2, rows, 128).transpose(0, 2, 1, 3)
    return result.reshape(nz, rows, columns)


def solution(mesh):
    return jax.shard_map(
        body,
        mesh=mesh,
        in_specs=(P(None, "lat", "lon"), P("lat", "lon"), P("lat", "lon"), P(), P(), P(), P()),
        out_specs=P(None, "lat", "lon"),
        check_vma=False,
    )
```

```python
import functools

import jax
import jax.numpy as jnp
from jax import lax
from jax.experimental import pallas as pl
from jax.experimental.pallas import tpu as pltpu
from jax.sharding import PartitionSpec as P

STEPS = 4
HALO = 16
CHUNKS = 2
F32 = jnp.float32
BF16 = jnp.bfloat16
MESH = pl.DeviceIdType.MESH


def split(value):
    high = value.astype(BF16)
    return high, (value - high.astype(F32)).astype(BF16)


def dot(left, right):
    return jnp.dot(left, right, preferred_element_type=F32)


def band(distance, width):
    u = jnp.maximum(2.0 * width - 1.0 - jnp.abs(distance), 0.0)
    v = jnp.maximum(u - width, 0.0)
    return u * (u + 1.0) * (u + 2.0) - 4.0 * (v * (v + 1.0) * (v + 2.0))


def diffuse(rows, faces):
    for step in range(STEPS):
        flux = [faces[step + m] * (rows[m + 1] - rows[m]) for m in range(len(rows) - 1)]
        rows = [rows[m] + (flux[m] - flux[m - 1]) for m in range(1, len(rows) - 1)]
    return rows


def kernel(
    band_hbm, inc_hbm, sea_hbm, cell_hbm, sigma_hbm, diff_hbm, root_hbm, out_ref,
    band_ref, sea_ref, cell_ref, sigma_ref, diff_ref, root_ref,
    inc_ref, first, second, mid, fin, edge, halo, other, faces_ref, w_high, w_low, zscale, halos, sums,
    load_sem, send_edge, recv_edge, send_corner, recv_corner, send_lat, recv_lat,
):
    nz = root_ref.shape[0]
    lat_total = diff_ref.shape[1]
    part = nz // CHUNKS
    lat_count, lon_count = lax.axis_size("lat"), lax.axis_size("lon")
    lat, lon = lax.axis_index("lat"), lax.axis_index("lon")
    north, south = lax.rem(lat + 1, lat_count), lax.rem(lat + lat_count - 1, lat_count)
    east, west = lax.rem(lon + 1, lon_count), lax.rem(lon + lon_count - 1, lon_count)

    loads = [
        pltpu.make_async_copy(inc_hbm.at[:, pl.ds(128 * h, 128)], inc_ref.at[h], load_sem.at[h])
        for h in range(2)
    ]
    for i, (source, target) in enumerate(
        (
            (root_hbm, root_ref), (sigma_hbm, sigma_ref), (sea_hbm, sea_ref), (cell_hbm, cell_ref),
            (diff_hbm, diff_ref), (band_hbm, band_ref),
        )
    ):
        loads.append(pltpu.make_async_copy(source, target, load_sem.at[2 + i]))
    for load in loads:
        load.start()
    has_south, has_north = lat > 0, lat < lat_count - 1
    barrier = pltpu.get_barrier_semaphore()

    def greet(a, columns):
        for o in columns:
            pl.semaphore_signal(barrier, inc=1, device_id={"lat": a, "lon": o}, device_id_type=MESH)

    greet(lat, (east, west))
    pl.when(has_south)(lambda: greet(south, (lon, east, west)))
    pl.when(has_north)(lambda: greet(north, (lon, east, west)))

    loads[2].wait()
    loads[3].wait()
    lift = root_ref[...].T * sigma_ref[...]
    lift_high, lift_low = split(lift)
    lift3 = jnp.concatenate([lift_high, lift_high, lift_low], axis=1)
    lower_high, lower_low = split(lift.T)
    lower3 = []
    for c in range(CHUNKS):
        high, low = (x[:, c * part : (c + 1) * part] for x in (lower_high, lower_low))
        lower3.append(jnp.concatenate([high, high, low], axis=1))

    level = lax.broadcasted_iota(jnp.int32, (nz, 256), 0)
    lane128 = lax.broadcasted_iota(jnp.int32, (nz, 128), 1)

    for load in loads[4:6] + loads[:2]:
        load.wait()
    left_pack = jnp.zeros((nz, 128), F32)
    right_pack = jnp.zeros((nz, 128), F32)
    for j in range(8):
        sea = level < sea_ref[j : j + 1, :]
        raw = jnp.concatenate([inc_ref[h, pl.ds(j, nz, stride=8), :] for h in range(2)], axis=1)
        start = jnp.where(sea, raw * cell_ref[j : j + 1, :], 0.0)
        high, low = split(start)
        lifted = dot(lift3, jnp.concatenate([high, low, high], axis=0))
        for c in range(CHUNKS):
            first[c, 8 + j] = lifted[c * part : (c + 1) * part]
        mine = (lane128 >= HALO * j) & (lane128 < HALO * (j + 1))
        left = pltpu.roll(lifted[:, :128], HALO * j, 1) if j else lifted[:, :128]
        shift = (HALO * j - 112) % 128
        right = pltpu.roll(lifted[:, 128:], shift, 1) if shift else lifted[:, 128:]
        left_pack = jnp.where(mine, left, left_pack)
        right_pack = jnp.where(mine, right, right_pack)
    edge[0] = left_pack
    edge[1] = right_pack

    @pl.when(jnp.logical_not(has_south))
    def _():
        first[:, 0:8] = jnp.zeros_like(first[:, 0:8])
        other[:, 1] = jnp.zeros_like(other[:, 1])

    @pl.when(jnp.logical_not(has_north))
    def _():
        first[:, 16:24] = jnp.zeros_like(first[:, 16:24])
        other[:, 0] = jnp.zeros_like(other[:, 0])

    def lat_copy(c, way, a):
        return pltpu.make_async_remote_copy(
            src_ref=first.at[c, pl.ds(8, 8)],
            dst_ref=first.at[c, pl.ds(16 * way, 8)],
            send_sem=send_lat.at[c, way],
            recv_sem=recv_lat.at[c, way],
            device_id={"lat": a, "lon": lon},
            device_id_type=MESH,
        )

    def send_rows(c):
        pl.when(has_north)(lambda: lat_copy(c, 0, north).start())
        pl.when(has_south)(lambda: lat_copy(c, 1, south).start())

    inside = has_south.astype(jnp.int32) + has_north.astype(jnp.int32)
    pl.semaphore_wait(barrier, 2 + 3 * inside)
    edge_copies = []
    for side, o in ((0, west), (1, east)):
        copy = pltpu.make_async_remote_copy(
            src_ref=edge.at[side],
            dst_ref=halo.at[1 - side],
            send_sem=send_edge.at[side],
            recv_sem=recv_edge.at[1 - side],
            device_id={"lat": lat, "lon": o},
            device_id_type=MESH,
        )
        copy.start()
        edge_copies.append(copy)
    def corner_copies(way, a):
        return [
            pltpu.make_async_remote_copy(
                src_ref=edge.at[side],
                dst_ref=other.at[1 - side, way],
                send_sem=send_corner.at[side, way],
                recv_sem=recv_corner.at[1 - side, way],
                device_id={"lat": a, "lon": o},
                device_id_type=MESH,
            )
            for side, o in ((0, west), (1, east))
        ]

    def each(copies, action):
        for copy in copies:
            getattr(copy, action)()

    pl.when(has_south)(lambda: each(corner_copies(0, south), "start"))
    pl.when(has_north)(lambda: each(corner_copies(1, north), "start"))
    for c in range(CHUNKS):
        send_rows(c)

    for load in loads[6:]:
        load.wait()
    column = lax.broadcasted_iota(jnp.int32, (lat_total, 384), 0)
    block = lax.broadcasted_iota(jnp.int32, (lat_total, 384), 1) // HALO
    row = 8 * lat + jnp.where(block < 16, block, block - 24)
    pick = jnp.where((column == row) & (column < lat_total - 1), 1.0, 0.0).astype(BF16)
    d_high, rest = diff_ref[...].astype(BF16), None
    rest = diff_ref[...] - d_high.astype(F32)
    d_mid, d_low = split(rest)
    packed_faces = dot(d_high, pick) + dot(d_mid, pick) + dot(d_low, pick)
    for m in range(23):
        lane = HALO * ((m - 8) % 24)
        faces_ref[m] = jnp.broadcast_to(packed_faces[:, lane : lane + 1], (nz, 128))

    inner = (
        lax.broadcasted_iota(jnp.int32, (128, 128), 0) - lax.broadcasted_iota(jnp.int32, (128, 128), 1)
    ).astype(F32)
    outer = (
        lax.broadcasted_iota(jnp.int32, (HALO, 128), 0) - lax.broadcasted_iota(jnp.int32, (HALO, 128), 1)
    ).astype(F32)
    w_high[...] = jnp.zeros_like(w_high)
    w_low[...] = jnp.zeros_like(w_low)
    for q in range(16):
        j = (q - 4) % 8
        width = band_ref[lax.rem(8 * lat + (q - 4 + lat_total), lat_total)].astype(F32) + 1.0
        zscale[q] = 1.0 / jnp.full((1, 256), 6.0 * (width * width) * (width * width), F32)
        for ref, a, b, c in zip(
            (w_high, w_low),
            split(band(inner, width)),
            split(band(outer - 16.0, width)),
            split(band(outer + 128.0, width)),
        ):
            ref[q, 0:128, 0:128] = a
            ref[q, 128:256, 128:256] = a
            ref[q, 112:128, 128:256] = b
            ref[q, 256 + HALO * j : 272 + HALO * j, 0:128] = b
            ref[q, 128:144, 0:128] = c
            ref[q, 384 + HALO * j : 400 + HALO * j, 128:256] = c

    def halo_pass():
        each(edge_copies, "wait_recv")
        pl.when(has_north)(lambda: each(corner_copies(0, south), "wait_recv"))
        pl.when(has_south)(lambda: each(corner_copies(1, north), "wait_recv"))
        sides = []
        for side in range(2):
            field = jnp.concatenate([halo[side], other[side, 0], other[side, 1]], axis=1)
            for step in range(STEPS):
                flux = packed_faces * (pltpu.roll(field, 384 - HALO, 1) - field)
                field = field + (flux - pltpu.roll(flux, HALO, 1))
            sides.append(field)
        for v in range(3):
            halos[v, 0], halos[v, 1] = split(
                jnp.concatenate([field[:, 128 * v : 128 * v + 128] for field in sides], axis=1)
            )

    def rows_pass(buffer, c, base, face, store, offset):
        def group(g, carry):
            at = pl.multiple_of(g * 8, 8)
            whole = pl.multiple_of(c * part + g * 8, 8)
            faces = [faces_ref[face + m, pl.ds(whole, 8), :] for m in range(15)]
            for half in range(2):
                lanes = slice(128 * half, 128 * half + 128)
                rows = [buffer[c, base + m, pl.ds(at, 8), lanes] for m in range(16)]
                for j, value in enumerate(diffuse(rows, faces)):
                    store[offset + j, pl.ds(whole, 8), lanes] = value
            return carry

        lax.fori_loop(0, part // 8, group, 0, unroll=True)

    def zonal(c, half):
        levels = slice(c * part, (c + 1) * part)
        for i in range(8):
            q = 8 * half + i
            group = 2 - 2 * half if i < 4 else half
            high, low = split(mid[q, levels, :])
            high = jnp.concatenate([high, halos[group, 0, levels, :]], axis=1)
            low = jnp.concatenate([low, halos[group, 1, levels, :]], axis=1)
            both = dot(jnp.concatenate([high, low], axis=0), w_high[q])
            total = both[:part] + both[part:] + dot(high, w_low[q])
            second[c, q] = total * zscale[q]

    def receive(c, half):
        there = jnp.where(half == 0, lat, lat_count - 1 - lat) > 0
        pl.when(there)(lambda: lat_copy(c, half, north).wait_recv())
        rows_pass(first, c, 8 * half, 8 * half, mid, 8 * half)

    late = lax.rem(lat, 2)
    early = 1 - late
    for c in range(CHUNKS):
        receive(c, early)
    halo_pass()
    for c in range(CHUNKS):
        zonal(c, early)
    for c in range(CHUNKS):
        receive(c, late)
        zonal(c, late)
        rows_pass(second, c, 0, 4, fin, 0)
        for j in range(8):
            high, low = split(fin[j, c * part : (c + 1) * part, :])
            lowered = dot(lower3[c], jnp.concatenate([high, low, high], axis=0))
            if c:
                lowered = lowered + sums[j]
            if c < CHUNKS - 1:
                sums[j] = lowered
                continue
            sea = level < sea_ref[j : j + 1, :]
            result = jnp.where(sea, lowered * cell_ref[j : j + 1, :], 0.0)
            for h in range(2):
                out_ref[pl.ds(8 * h + j, nz, stride=16), :] = result[:, 128 * h : 128 * h + 128]

    each(edge_copies, "wait_send")

    def sent(corner_way, a, way):
        each(corner_copies(corner_way, a), "wait_send")
        each([lat_copy(c, way, a) for c in range(CHUNKS)], "wait_send")

    pl.when(has_south)(lambda: sent(0, south, 1))
    pl.when(has_north)(lambda: sent(1, north, 0))


def body(increment, sea_levels, cell_sigma, level_sigma, diffusivity, band_width, vertical_root):
    nz, rows, columns = increment.shape
    part = nz // CHUNKS
    result = pl.pallas_call(
        kernel,
        out_shape=jax.ShapeDtypeStruct((2 * nz * rows, 128), F32),
        in_specs=[
            pl.BlockSpec(memory_space=pl.ANY)
        ]
        * 7,
        out_specs=pl.BlockSpec(memory_space=pltpu.VMEM),
        scratch_shapes=[
            pltpu.SMEM(band_width.shape, jnp.int32),
            pltpu.VMEM(sea_levels.shape, jnp.int32),
            pltpu.VMEM(cell_sigma.shape, F32),
            pltpu.VMEM((1, nz), F32),
            pltpu.VMEM(diffusivity.shape, F32),
            pltpu.VMEM(vertical_root.shape, F32),
            pltpu.VMEM((2, nz * rows, 128), F32),
            pltpu.VMEM((CHUNKS, 24, part, columns), F32),
            pltpu.VMEM((CHUNKS, 16, part, columns), F32),
            pltpu.VMEM((16, nz, columns), F32),
            pltpu.VMEM((8, nz, columns), F32),
            pltpu.VMEM((2, nz, 128), F32),
            pltpu.VMEM((2, nz, 128), F32),
            pltpu.VMEM((2, 2, nz, 128), F32),
            pltpu.VMEM((23, nz, 128), F32),
            pltpu.VMEM((16, 512, 256), BF16),
            pltpu.VMEM((16, 512, 256), BF16),
            pltpu.VMEM((16, 1, 256), F32),
            pltpu.VMEM((3, 2, nz, columns), BF16),
            pltpu.VMEM((8, nz, columns), F32),
            pltpu.SemaphoreType.DMA((8,)),
            pltpu.SemaphoreType.DMA((2,)),
            pltpu.SemaphoreType.DMA((2,)),
            pltpu.SemaphoreType.DMA((2, 2)),
            pltpu.SemaphoreType.DMA((2, 2)),
            pltpu.SemaphoreType.DMA((CHUNKS, 2)),
            pltpu.SemaphoreType.DMA((CHUNKS, 2)),
        ],
        compiler_params=pltpu.CompilerParams(collective_id=0, has_side_effects=True, vmem_limit_bytes=24 * 2**20),
        name="covariance",
    )(*(pltpu.with_memory_space_constraint(x, pltpu.HBM) for x in (
        band_width,
        increment.reshape(nz * rows, columns),
        sea_levels,
        cell_sigma,
        level_sigma.reshape(1, nz),
        diffusivity,
        vertical_root,
    )))
    result = result.reshape(nz, 2, rows, 128).transpose(0, 2, 1, 3)
    return result.reshape(nz, rows, columns)


def solution(mesh):
    return jax.shard_map(
        body,
        mesh=mesh,
        in_specs=(P(None, "lat", "lon"), P("lat", "lon"), P("lat", "lon"), P(), P(), P(), P()),
        out_specs=P(None, "lat", "lon"),
        check_vma=False,
    )
```
